32 devices in a mesh: dp: 16 (over z, y, x), mp: 2 (over core).
Axes of the slice: x: 2, y: 2, z: 4, core: 2. Of those that a mesh axis runs over, the one named last changes fastest.
Arguments:
- log_rows: bfloat16 [98304, 256], P('dp'), may hold values from -6 to 6
- query_ids: int32 [98304], P('dp'), may hold values from 0 to 191, as said below
- doc_ranks: int32 [98304], P('dp'), may hold values from 0 to 511, as said below
- row_counts: int32 [16, 16], P('dp'), may hold values from 0 to 384, as said below
- list_lengths: int32 [192], P('dp'), may hold values from 64 to 512, as said below
- gains: float32 [192, 512], P('dp'), may hold values from 0.01 to 1
- weight_in: float32 [256, 4096], P(None, 'mp'), may hold values from -0.375 to 0.375
- bias_in: float32 [4096], P('mp'), may hold values from -3 to 3
- weight_out: float32 [4096], P('mp'), may hold values from -0.3 to 0.3
- moment_w: float32 [256, 4096], P(None, 'mp'), may hold values from -0.6 to 0.6
- second_w: float32 [256, 4096], P(None, 'mp'), may hold values from 0.05 to 2
- moment_b: float32 [4096], P('mp'), may hold values from -0.6 to 0.6
- second_b: float32 [4096], P('mp'), may hold values from 0.05 to 2
- moment_o: float32 [4096], P('mp'), may hold values from -0.6 to 0.6
- second_o: float32 [4096], P('mp'), may hold values from 0.05 to 2
Outputs:
- doc_lambdas: float32 [192, 512], P('dp')
- weight_in_next: float32 [256, 4096], P(None, 'mp')
- moment_w_next: float32 [256, 4096], P(None, 'mp')
- second_w_next: float32 [256, 4096], P(None, 'mp')
- bias_in_next: float32 [4096], P('mp')
- moment_b_next: float32 [4096], P('mp')
- second_b_next: float32 [4096], P('mp')
- weight_out_next: float32 [4096], P('mp')
- moment_o_next: float32 [4096], P('mp')
- second_o_next: float32 [4096], P('mp')
The draws below stay inside these ranges and needn't reach their ends.
Inputs may be any that keep to these rules, and one draw needn't show every extreme that they name: row_counts[s, j] is at most 384; the live rows that all shards hold for owner j number list_lengths summed over owner j's queries j * 12 to j * 12 + 11; some owner receives 384 live rows from every shard. `query_ids`: A live row of the block for owner j belongs to one of owner j's queries; rows that are not live carry arbitrary ids. `doc_ranks`: the live rows of query q carry the ranks 0 to list_lengths[q] - 1, each once; rows that are not live carry arbitrary ranks. `list_lengths`: every owner has a list of 512 documents.
All inputs are finite; a program needn't handle non-finite values.
Results may differ from the reference program's by a relative error of at most 0.0049.
Values may be sent and summed in bfloat16 or wider, within the bound.
A program may use at most 192 MiB of HBM per device.

```python
import math
import jax
import jax.numpy as jnp
from jax import lax

F = 256
H = 4096
LIST = 512
Q_DEV = 12
QUERIES = 192
CAP = 384
LOG_DEV = 6144
N_DP = 16


def layout(key):
    shard_count = QUERIES // Q_DEV
    key = jax.random.fold_in(key, 11)
    subkeys = jax.random.split(key, 8)
    owners = jnp.arange(shard_count)
    list_index = jnp.arange(Q_DEV)
    lengths = jax.random.randint(subkeys[0], (shard_count, Q_DEV), LIST // 8, LIST + 1)
    longest = jax.random.randint(subkeys[1], (shard_count,), 0, Q_DEV)
    lengths = jnp.where(list_index[None, :] == longest[:, None], LIST, lengths)
    full_owner = jax.random.randint(subkeys[2], (), 0, shard_count)
    lengths = jnp.where(owners[:, None] == full_owner, LIST, lengths)
    short_owner = (full_owner + 1 + jax.random.randint(subkeys[3], (), 0, shard_count - 1)) % shard_count
    short_list = (longest[short_owner] + 1) % Q_DEV
    lengths = jnp.where((owners[:, None] == short_owner) & (list_index[None, :] == short_list), LIST // 8, lengths)
    totals = jnp.sum(lengths, axis=1)
    order_keys = jax.random.randint(subkeys[4], (shard_count, shard_count), 0, 1 << 20) * shard_count + owners[None, :]
    source_order = jnp.argsort(order_keys, axis=1)
    position = jnp.argsort(source_order, axis=1)
    counts = jnp.clip(totals[:, None] - CAP * position, 0, CAP).T
    row_index = jnp.arange(CAP)
    doc_index = position.T[:, :, None] * CAP + row_index[None, None, :]
    starts = jnp.cumsum(lengths, axis=1) - lengths
    list_of_doc = jnp.sum((doc_index[..., None] >= starts[None, :, None, 1:]).astype(jnp.int32), axis=-1)
    inner_pos = doc_index - starts.reshape(-1)[owners[None, :, None] * Q_DEV + list_of_doc]
    shuffle_keys = jax.random.randint(subkeys[5], (QUERIES, LIST), 0, 1 << 20) * LIST + jnp.arange(LIST)[None, :]
    shuffled = jnp.argsort(shuffle_keys, axis=1)
    is_kept = shuffled < lengths.reshape(-1)[:, None]
    kept_first = jnp.argsort(jnp.where(is_kept, 0, 1) * LIST + jnp.arange(LIST)[None, :], axis=1)
    rank_table = jnp.take_along_axis(shuffled, kept_first, axis=1)
    live_query = owners[None, :, None] * Q_DEV + list_of_doc
    table_index = live_query * LIST + jnp.clip(inner_pos, 0, LIST - 1)
    live_rank = rank_table.reshape(-1)[table_index]
    is_live = row_index[None, None, :] < counts[:, :, None]
    pad_query = jax.random.randint(subkeys[6], is_live.shape, 0, QUERIES)
    pad_rank = jax.random.randint(subkeys[7], is_live.shape, 0, LIST)
    query_out = jnp.where(is_live, live_query, pad_query).astype(jnp.int32)
    rank_out = jnp.where(is_live, live_rank, pad_rank).astype(jnp.int32)
    return (counts.astype(jnp.int32), query_out.reshape(-1), rank_out.reshape(-1), lengths.reshape(-1).astype(jnp.int32))


def draw_row_counts(key, part):
    return layout(key)[0]


def draw_query_ids(key, part):
    return layout(key)[1]


def draw_doc_ranks(key, part):
    return layout(key)[2]


def draw_list_lengths(key, part):
    return layout(key)[3]


def levels(key, dims, shards, least, largest):
    def one(dim, shards_of):
        heights = jax.random.uniform(jax.random.fold_in(jax.random.fold_in(key, 6), dim), (shards_of,), jnp.float32, least / len(shards), largest / len(shards))
        return jnp.repeat(jnp.exp(heights), dims[dim] // shards_of).reshape((-1,) + (1,) * (len(dims) - dim - 1))

    factor_of = one(*shards[0])
    for cut in shards[1:]:
        factor_of = factor_of * one(*cut)
    return factor_of


def bell_draw(key, extent, width, limit, cuts=(), dtype=jnp.bfloat16):
    array = width * jax.random.normal(key, extent, jnp.float32)
    if cuts:
        array = array * levels(key, extent, cuts, -0.22, 0.18)
    return jnp.clip(array, -limit, limit).astype(dtype)


def setup_inputs(seed: int = 0) -> dict:
    key_list = jax.random.split(jax.random.key(seed), 16)
    return {
        "log_rows": bell_draw(key_list[0], (N_DP * LOG_DEV, F), 1.0, 6.0, ((0, 16),)),
        "query_ids": draw_query_ids(jax.random.fold_in(key_list[15], 71), 0),
        "doc_ranks": draw_doc_ranks(jax.random.fold_in(key_list[15], 71), 0),
        "row_counts": draw_row_counts(jax.random.fold_in(key_list[15], 71), 0),
        "list_lengths": draw_list_lengths(jax.random.fold_in(key_list[15], 71), 0),
        "gains": jnp.clip(jnp.exp(math.log(1.0) - 4.6051702 * jax.random.uniform(key_list[5], (QUERIES, LIST), jnp.float32) ** levels(key_list[5], (QUERIES, LIST), ((0, 16),), -0.2, 0.2)), 0.01, 1.0),
        "weight_in": bell_draw(key_list[6], (F, H), F ** -0.5, 0.375, ((1, 2),), jnp.float32),
        "bias_in": bell_draw(key_list[7], (H,), 0.5, 3.0, ((0, 2),), jnp.float32),
        "weight_out": bell_draw(key_list[8], (H,), 0.05, 0.3, ((0, 2),), jnp.float32),
        "moment_w": bell_draw(key_list[9], (F, H), 0.1, 0.6, ((1, 2),), jnp.float32),
        "second_w": jnp.clip(jnp.exp(math.log(2.0) - 3.6888794 * jax.random.uniform(key_list[10], (F, H), jnp.float32) ** levels(key_list[10], (F, H), ((1, 2),), -0.2, 0.2)), 0.05, 2.0),
        "moment_b": bell_draw(key_list[11], (H,), 0.1, 0.6, ((0, 2),), jnp.float32),
        "second_b": jnp.clip(jnp.exp(math.log(2.0) - 3.6888794 * jax.random.uniform(key_list[12], (H,), jnp.float32) ** levels(key_list[12], (H,), ((0, 2),), -0.2, 0.2)), 0.05, 2.0),
        "moment_o": bell_draw(key_list[13], (H,), 0.1, 0.6, ((0, 2),), jnp.float32),
        "second_o": jnp.clip(jnp.exp(math.log(2.0) - 3.6888794 * jax.random.uniform(key_list[14], (H,), jnp.float32) ** levels(key_list[14], (H,), ((0, 2),), -0.2, 0.2)), 0.05, 2.0),
    }


beta_one = 0.9
beta_two = 0.95
learn_rate = 0.001
adam_eps = 1e-08

def gelu_tanh(values):
    return jax.nn.gelu(values, approximate=True)

def list_lambdas(score_rows, gain_rows, lengths):
    list_width = gain_rows.shape[1]
    positions = jnp.arange(list_width)
    discount = 1.0 / jnp.log2(2.0 + positions.astype(jnp.float32))
    keep_mask = (positions[None, :] < lengths[:, None]).astype(jnp.float32)

    def per_list(triple):
        row_score, row_gain, row_keep = triple
        delta_s = row_score[:, None] - row_score[None, :]
        delta_g = row_gain[:, None] - row_gain[None, :]
        weight = jnp.abs(discount[:, None] - discount[None, :]) * row_keep[:, None] * row_keep[None, :]
        pair_term = jnp.maximum(delta_g, 0.0) * jax.nn.sigmoid(-delta_s) - jnp.maximum(-delta_g, 0.0) * jax.nn.sigmoid(delta_s)
        return -lax.optimization_barrier(jnp.sum(weight * pair_term, axis=1))
    return lax.map(per_list, (score_rows, gain_rows, keep_mask))

def adam_step(weights, moment, second, gradient):
    moment_next = beta_one * moment + (1.0 - beta_one) * gradient
    second_next = beta_two * second + (1.0 - beta_two) * gradient * gradient
    weights_next = weights - learn_rate * moment_next / (jnp.sqrt(second_next) + adam_eps)
    return (weights_next, moment_next, second_next)

def reference(log_rows, query_ids, doc_ranks, row_counts, list_lengths, gains, weight_in, bias_in, weight_out, moment_w, second_w, moment_b, second_b, moment_o, second_o):
    shard_count = QUERIES // Q_DEV
    owner_rows = Q_DEV * LIST
    blocks = log_rows.reshape(shard_count, shard_count, CAP, F)
    is_live = jnp.arange(CAP)[None, None, :] < row_counts[:, :, None]
    slot_index = jnp.where(is_live, query_ids.reshape(shard_count, shard_count, CAP) % Q_DEV * LIST + doc_ranks.reshape(shard_count, shard_count, CAP), owner_rows)
    w_low = weight_in.astype(jnp.bfloat16)
    per_owner_inputs = (jnp.swapaxes(blocks, 0, 1), jnp.swapaxes(slot_index, 0, 1), list_lengths.reshape(shard_count, Q_DEV), gains.reshape(shard_count, Q_DEV, LIST))

    def per_owner(totals, pieces):
        owner_blocks, owner_slots, owner_lengths, owner_gains = pieces
        placed = jnp.zeros((owner_rows, F), jnp.bfloat16).at[owner_slots.reshape(-1)].set(owner_blocks.reshape(-1, F), mode='drop')
        pre_act = jnp.dot(placed, w_low, preferred_element_type=jnp.float32) + bias_in
        hidden, gelu_back = jax.vjp(gelu_tanh, pre_act)
        scores = lax.optimization_barrier(jnp.sum(hidden * weight_out, axis=1))
        lambdas = list_lambdas(scores.reshape(Q_DEV, LIST), owner_gains, owner_lengths)
        row_lambdas = lambdas.reshape(-1) / QUERIES
        grad_pre = gelu_back(row_lambdas[:, None] * weight_out)[0]
        grad_w = lax.dot_general(placed, grad_pre.astype(jnp.bfloat16), (((0,), (0,)), ((), ())), preferred_element_type=jnp.float32)
        grad_b = lax.optimization_barrier(jnp.sum(grad_pre, axis=0))
        grad_o = lax.optimization_barrier(jnp.sum(row_lambdas[:, None] * hidden, axis=0))
        return ((totals[0] + grad_w, totals[1] + grad_b, totals[2] + grad_o), lambdas)
    start_totals = (jnp.zeros((F, H), jnp.float32), jnp.zeros((H,), jnp.float32), jnp.zeros((H,), jnp.float32))
    sums, lambdas = lax.scan(per_owner, start_totals, per_owner_inputs)
    doc_lambdas = lambdas.reshape(QUERIES, LIST)
    weight_next, moment_w_next, second_w_next = adam_step(weight_in, moment_w, second_w, sums[0])
    bias_next, moment_b_next, second_b_next = adam_step(bias_in, moment_b, second_b, sums[1])
    out_next, moment_o_next, second_o_next = adam_step(weight_out, moment_o, second_o, sums[2])
    return (doc_lambdas, weight_next, moment_w_next, second_w_next, bias_next, moment_b_next, second_b_next, out_next, moment_o_next, second_o_next)
```

```python
import functools
import math

import jax
import jax.numpy as jnp
from jax import lax
from jax.experimental import pallas as pl
from jax.experimental.pallas import tpu as pltpu
from jax.sharding import PartitionSpec as P

beta_one = 0.9
beta_two = 0.95
learn_rate = 0.001
adam_eps = 1e-08

C0 = math.sqrt(2.0 / math.pi)
C1 = C0 * 0.044715
MESH = pl.DeviceIdType.MESH
LANES = 128
BLOCK = 512
BF = jnp.bfloat16
F32 = jnp.float32


def fwd_kernel(x_ref, w_ref, b_ref, wo_ref, h_ref, g_ref, s_ref):
    x = x_ref[...]
    hidden = w_ref.shape[1]
    step = 256
    acc = jnp.zeros((x.shape[0], LANES), F32)
    for c in range(0, hidden, step):
        v = jnp.dot(x, w_ref[:, c : c + step], preferred_element_type=F32) + b_ref[:, c : c + step]
        v2 = v * v
        s = 0.5 * jnp.tanh(v * (C1 * v2 + C0)) + 0.5
        h = v * s
        g = s + (h * (1.0 - s)) * ((6.0 * C1) * v2 + 2.0 * C0)
        hb = h.astype(BF)
        h_ref[:, c : c + step] = hb
        g_ref[:, c : c + step] = g.astype(BF)
        acc = acc + jnp.dot(hb, wo_ref[c : c + step, :], preferred_element_type=F32)
    s_ref[0] = jnp.sum(acc.T, axis=0, keepdims=True)


def forward(rows, w_low, bias, wo_pair):
    total, features = rows.shape
    hidden = w_low.shape[1]
    blocks = total // BLOCK
    return pl.pallas_call(
        fwd_kernel,
        grid=(blocks,),
        in_specs=[
            pl.BlockSpec((BLOCK, features), lambda i: (i, 0)),
            pl.BlockSpec((features, hidden), lambda i: (0, 0)),
            pl.BlockSpec((1, hidden), lambda i: (0, 0)),
            pl.BlockSpec((hidden, LANES), lambda i: (0, 0)),
        ],
        out_specs=[
            pl.BlockSpec((BLOCK, hidden), lambda i: (i, 0)),
            pl.BlockSpec((BLOCK, hidden), lambda i: (i, 0)),
            pl.BlockSpec((1, 1, BLOCK), lambda i: (i, 0, 0)),
        ],
        out_shape=[
            jax.ShapeDtypeStruct((total, hidden), BF),
            jax.ShapeDtypeStruct((total, hidden), BF),
            jax.ShapeDtypeStruct((blocks, 1, BLOCK), F32),
        ],
        compiler_params=pltpu.CompilerParams(vmem_limit_bytes=48 << 20),
    )(rows, w_low, bias, wo_pair)


def split_three(values):
    first = values.astype(BF)
    rest = values - first.astype(F32)
    second = rest.astype(BF)
    third = (rest - second.astype(F32)).astype(BF)
    return first, second, third


def mid_kernel(
    n, scale, msg_ref, gain_ref, keep_ref, weight_ref,
    doc_ref, lam_ref,
    arrive, lam_out, lam_in, s_row, l_row, s_col, g_col, lam_t,
    send_a, recv_a, send_l, recv_l,
):
    me = lax.axis_index("dp")
    core = lax.axis_index("mp")
    other = 1 - core
    high_rows = gain_ref.shape[0]
    per_list = weight_ref.shape[0]
    lists = high_rows // per_list
    cap = msg_ref.shape[2]

    barrier = pltpu.get_barrier_semaphore()

    @pl.loop(1, n)
    def _(k):
        peer = lax.rem(me + k, n)
        pl.semaphore_signal(barrier, inc=1, device_id=(peer, core), device_id_type=MESH)
        pl.semaphore_signal(barrier, inc=1, device_id=(peer, other), device_id_type=MESH)

    pl.semaphore_signal(barrier, inc=1, device_id=(me, other), device_id_type=MESH)
    pl.semaphore_wait(barrier, 2 * n - 1)

    def score_copy(peer, to_core, side):
        return pltpu.make_async_remote_copy(
            src_ref=msg_ref.at[peer],
            dst_ref=arrive.at[core, me],
            send_sem=send_a.at[side, peer],
            recv_sem=recv_a.at[core, me],
            device_id=(peer, to_core),
            device_id_type=MESH,
        )

    def arrival(from_core, peer):
        return pltpu.make_async_remote_copy(
            src_ref=msg_ref.at[peer],
            dst_ref=arrive.at[from_core, peer],
            send_sem=send_a.at[0, peer],
            recv_sem=recv_a.at[from_core, peer],
            device_id=(peer, from_core),
            device_id_type=MESH,
        )

    @pl.loop(1, n)
    def _(k):
        peer = lax.rem(me + k, n)
        score_copy(peer, core, 0).start()
        score_copy(peer, other, 1).start()

    score_copy(me, other, 1).start()
    arrive[core, me] = msg_ref[me]

    high_iota = lax.broadcasted_iota(jnp.int32, (LANES, cap), 0).astype(F32)

    def absorb(shard, total):
        one = arrive[0, shard]
        two = arrive[1, shard]
        value = one[0:1] + two[0:1]
        low = (one[2:3] == high_iota).astype(F32).astype(BF)
        at_high = one[1:2] == high_iota[:high_rows]
        for piece in split_three(value):
            spread = jnp.where(at_high, piece.astype(F32), 0.0).astype(BF)
            total = total + lax.dot_general(
                spread, low, (((1,), (1,)), ((), ())), preferred_element_type=F32
            )
        return total

    arrival(other, me).wait_recv()
    total = absorb(me, jnp.zeros((high_rows, LANES), F32))

    def take(k, total):
        peer = lax.rem(me + k, n)
        arrival(0, peer).wait_recv()
        arrival(1, peer).wait_recv()
        return absorb(peer, total)

    total = lax.fori_loop(1, n, take, total)
    scores = jnp.where(keep_ref[...] > 0.0, 0.5 * total, -1e30)
    s_row[...] = scores
    padding = jnp.zeros((LANES - high_rows, LANES), F32)
    s_turn = jnp.concatenate([scores, padding], axis=0).T
    g_turn = jnp.concatenate([gain_ref[...], padding], axis=0).T
    for i in range(high_rows):
        s_col[i] = s_turn[:, i : i + 1]
        g_col[i] = g_turn[:, i : i + 1]

    def one_list(q, carry):
        base = q * per_list
        row_s = jnp.concatenate([s_row[pl.ds(base + k, 1), :] for k in range(per_list)], axis=1)
        row_g = jnp.concatenate([gain_ref[pl.ds(base + k, 1), :] for k in range(per_list)], axis=1)
        sums = jnp.zeros((8, row_s.shape[1]), F32)
        for k in range(per_list):
            col_s = s_col[base + k]
            col_g = g_col[base + k]
            for r in range(0, LANES, 8):
                delta_g = col_g[r : r + 8] - row_g
                delta_t = jnp.tanh(col_s[r : r + 8] - row_s)
                sums = sums + weight_ref[k, r : r + 8, :] * (delta_g - jnp.abs(delta_g) * delta_t)
        lam = 0.5 * jnp.sum(sums, axis=0, keepdims=True)
        for k in range(per_list):
            l_row[pl.ds(base + k, 1), :] = lam[:, k * LANES : (k + 1) * LANES]
        return carry

    lax.fori_loop(0, lists, one_list, 0)
    doc_ref[...] = l_row[...]
    turned = jnp.concatenate([l_row[...] * scale, padding], axis=0).T
    pieces = split_three(turned)
    for i in range(3):
        lam_t[i] = pieces[i]

    def answer(shard):
        info = arrive[core, shard]
        low = info[2:3] == high_iota
        high = (info[1:2] == high_iota).astype(F32).astype(BF)
        spread = jnp.dot(lam_t[0], high, preferred_element_type=F32)
        spread += jnp.dot(lam_t[1], high, preferred_element_type=F32)
        spread += jnp.dot(lam_t[2], high, preferred_element_type=F32)
        return jnp.sum(jnp.where(low, spread, 0.0), axis=0, keepdims=True)

    def lam_copy(peer):
        return pltpu.make_async_remote_copy(
            src_ref=lam_out.at[peer],
            dst_ref=lam_in.at[me],
            send_sem=send_l.at[peer],
            recv_sem=recv_l.at[me],
            device_id=(peer, core),
            device_id_type=MESH,
        )

    def lam_arrival(peer):
        return pltpu.make_async_remote_copy(
            src_ref=lam_out.at[peer],
            dst_ref=lam_in.at[peer],
            send_sem=send_l.at[peer],
            recv_sem=recv_l.at[peer],
            device_id=(peer, core),
            device_id_type=MESH,
        )

    @pl.loop(1, n)
    def _(k):
        peer = lax.rem(me + k, n)
        lam_out[peer] = answer(peer)
        lam_copy(peer).start()

    lam_ref[me] = answer(me)

    @pl.loop(1, n)
    def _(k):
        peer = lax.rem(me + k, n)
        lam_arrival(peer).wait_recv()
        lam_ref[peer] = lam_in[peer]

    @pl.loop(1, n)
    def _(k):
        peer = lax.rem(me + k, n)
        score_copy(peer, core, 0).wait_send()
        score_copy(peer, other, 1).wait_send()
        lam_copy(peer).wait_send()

    score_copy(me, other, 1).wait_send()


def middle(n, message, gain_rows, keep_rows, weights, query_total):
    cap = message.shape[2]
    high_rows = gain_rows.shape[0]
    vmem = pl.BlockSpec(memory_space=pltpu.VMEM)
    return pl.pallas_call(
        functools.partial(mid_kernel, n, 1.0 / query_total),
        in_specs=[vmem] * 4,
        out_specs=[vmem] * 2,
        out_shape=[
            jax.ShapeDtypeStruct((high_rows, LANES), F32),
            jax.ShapeDtypeStruct((n, 1, cap), F32),
        ],
        scratch_shapes=[
            pltpu.VMEM((2, n, 3, cap), F32),
            pltpu.VMEM((n, 1, cap), F32),
            pltpu.VMEM((n, 1, cap), F32),
            pltpu.VMEM((high_rows, LANES), F32),
            pltpu.VMEM((high_rows, LANES), F32),
            pltpu.VMEM((high_rows, LANES, 1), F32),
            pltpu.VMEM((high_rows, LANES, 1), F32),
            pltpu.VMEM((3, LANES, LANES), BF),
            pltpu.SemaphoreType.DMA((2, n)),
            pltpu.SemaphoreType.DMA((2, n)),
            pltpu.SemaphoreType.DMA((n,)),
            pltpu.SemaphoreType.DMA((n,)),
        ],
        compiler_params=pltpu.CompilerParams(
            collective_id=0, has_side_effects=True, vmem_limit_bytes=48 << 20
        ),
    )(message, gain_rows, keep_rows, weights)


def bwd_kernel(x_ref, h_ref, g_ref, lam_ref, wo_ref, out_ref, acc, acc_o):
    step = pl.program_id(0)
    features = x_ref.shape[1]
    hidden = h_ref.shape[1]
    chunk = 256

    @pl.when(step == 0)
    def _():
        acc[...] = jnp.zeros_like(acc)
        acc_o[...] = jnp.zeros_like(acc_o)

    lam = lam_ref[0]
    top = lam.astype(BF).astype(F32)
    place = lax.broadcasted_iota(jnp.int32, (16, lam.shape[1]), 0)
    pair = jnp.where(place == 0, top, jnp.where(place == 1, lam - top, 0.0)).astype(BF)
    scaled = (x_ref[...].astype(F32).T * lam).astype(BF)
    left = jnp.concatenate([scaled, pair], axis=0)
    for c in range(0, hidden, chunk):
        acc[:, c : c + chunk] += jnp.dot(left, g_ref[:, c : c + chunk], preferred_element_type=F32)
        acc_o[:, c : c + chunk] += jnp.dot(pair, h_ref[:, c : c + chunk], preferred_element_type=F32)

    @pl.when(step == pl.num_programs(0) - 1)
    def _():
        spot = lax.broadcasted_iota(jnp.int32, (16, LANES), 0)
        rest = out_ref.shape[1] - features - 16
        for k in range(hidden // LANES):
            cols = slice(k * LANES, (k + 1) * LANES)
            wo = wo_ref[:, cols]
            out_ref[k, :features, :] = (acc[:features, cols] * wo).astype(BF)
            grad_b = jnp.sum(acc[features:, cols], axis=0, keepdims=True) * wo
            grad_o = jnp.sum(acc_o[:, cols], axis=0, keepdims=True)
            tail = jnp.where(spot == 0, grad_b, jnp.where(spot == 1, grad_o, 0.0))
            out_ref[k, features : features + 16, :] = tail.astype(BF)
            if rest:
                out_ref[k, features + 16 :, :] = jnp.zeros((rest, LANES), BF)


def backward(rows, hid, slope, lam, wo_row, padded):
    total, features = rows.shape
    hidden = hid.shape[1]
    return pl.pallas_call(
        bwd_kernel,
        grid=(total // BLOCK,),
        in_specs=[
            pl.BlockSpec((BLOCK, features), lambda i: (i, 0)),
            pl.BlockSpec((BLOCK, hidden), lambda i: (i, 0)),
            pl.BlockSpec((BLOCK, hidden), lambda i: (i, 0)),
            pl.BlockSpec((1, 1, BLOCK), lambda i: (i, 0, 0)),
            pl.BlockSpec((1, hidden), lambda i: (0, 0)),
        ],
        out_specs=pl.BlockSpec((hidden // LANES, padded, LANES), lambda i: (0, 0, 0)),
        out_shape=jax.ShapeDtypeStruct((hidden // LANES, padded, LANES), BF),
        scratch_shapes=[
            pltpu.VMEM((features + 16, hidden), F32),
            pltpu.VMEM((16, hidden), F32),
        ],
        compiler_params=pltpu.CompilerParams(vmem_limit_bytes=48 << 20),
    )(rows, hid, slope, lam, wo_row)


def sum_kernel(n, in_ref, out_ref, arrive, mine, full, send_a, recv_a, send_b, recv_b):
    me = lax.axis_index("dp")
    core = lax.axis_index("mp")
    barrier = pltpu.get_barrier_semaphore()

    @pl.loop(1, n)
    def _(k):
        peer = lax.rem(me + k, n)
        pl.semaphore_signal(barrier, inc=1, device_id=(peer, core), device_id_type=MESH)

    pl.semaphore_wait(barrier, n - 1)

    def copy(source, target, sends, recvs, peer, slot):
        return pltpu.make_async_remote_copy(
            src_ref=source,
            dst_ref=target.at[slot],
            send_sem=sends.at[peer],
            recv_sem=recvs.at[slot],
            device_id=(peer, core),
            device_id_type=MESH,
        )

    @pl.loop(1, n)
    def _(k):
        peer = lax.rem(me + k, n)
        copy(in_ref.at[peer], arrive, send_a, recv_a, peer, me).start()

    def take(k, total):
        peer = lax.rem(me + n - k, n)
        copy(in_ref.at[peer], arrive, send_a, recv_a, peer, peer).wait_recv()
        return total + arrive[peer].astype(F32)

    total = lax.fori_loop(1, n, take, in_ref[me].astype(F32))
    mine[...] = total.astype(BF)

    @pl.loop(1, n)
    def _(k):
        peer = lax.rem(me + k, n)
        copy(mine, full, send_b, recv_b, peer, me).start()

    out_ref[me] = mine[...]

    @pl.loop(1, n)
    def _(k):
        peer = lax.rem(me + n - k, n)
        copy(mine, full, send_b, recv_b, peer, peer).wait_recv()
        out_ref[peer] = full[peer]

    @pl.loop(1, n)
    def _(k):
        peer = lax.rem(me + k, n)
        copy(in_ref.at[peer], arrive, send_a, recv_a, peer, me).wait_send()
        copy(mine, full, send_b, recv_b, peer, me).wait_send()


def sum_over_dp(n, parts):
    vmem = pl.BlockSpec(memory_space=pltpu.VMEM)
    return pl.pallas_call(
        functools.partial(sum_kernel, n),
        in_specs=[vmem],
        out_specs=vmem,
        out_shape=jax.ShapeDtypeStruct(parts.shape, BF),
        scratch_shapes=[
            pltpu.VMEM(parts.shape, BF),
            pltpu.VMEM(parts.shape[1:], BF),
            pltpu.VMEM(parts.shape, BF),
            pltpu.SemaphoreType.DMA((n,)),
            pltpu.SemaphoreType.DMA((n,)),
            pltpu.SemaphoreType.DMA((n,)),
            pltpu.SemaphoreType.DMA((n,)),
        ],
        compiler_params=pltpu.CompilerParams(
            collective_id=1, has_side_effects=True, vmem_limit_bytes=48 << 20
        ),
    )(parts)


def adam_step(weights, moment, second, gradient):
    moment_next = beta_one * moment + (1.0 - beta_one) * gradient
    second_next = beta_two * second + (1.0 - beta_two) * gradient * gradient
    weights_next = weights - learn_rate * moment_next / (jnp.sqrt(second_next) + adam_eps)
    return (weights_next, moment_next, second_next)


def adam_kernel(g_ref, w_ref, m_ref, s_ref, w_out, m_out, s_out):
    features = w_ref.shape[0]
    for k in range(g_ref.shape[0]):
        cols = slice(k * LANES, (k + 1) * LANES)
        grad = g_ref[k, :features, :].astype(F32)
        w_out[:, cols], m_out[:, cols], s_out[:, cols] = adam_step(
            w_ref[:, cols], m_ref[:, cols], s_ref[:, cols], grad
        )


def adam_matrix(grads, weights, moment, second):
    features, hidden = weights.shape
    group = 4
    block = pl.BlockSpec((features, group * LANES), lambda i: (0, i))
    return pl.pallas_call(
        adam_kernel,
        grid=(hidden // (group * LANES),),
        in_specs=[pl.BlockSpec((group,) + grads.shape[1:], lambda i: (i, 0, 0))] + [block] * 3,
        out_specs=[block] * 3,
        out_shape=[jax.ShapeDtypeStruct(weights.shape, F32)] * 3,
    )(grads, weights, moment, second)


def per_device(
    log_rows, query_ids, doc_ranks, row_counts, list_lengths, gains,
    weight_in, bias_in, weight_out, moment_w, second_w,
    moment_b, second_b, moment_o, second_o,
):
    n = lax.axis_size("dp")
    total, features = log_rows.shape
    cap = total // n
    hidden = weight_in.shape[1]
    list_count, list_width = gains.shape
    high_rows = list_count * list_width // LANES
    per_list = list_width // LANES

    is_live = jnp.arange(cap)[None, :] < row_counts.reshape(n, 1)
    slots = query_ids.reshape(n, cap) % list_count * list_width + doc_ranks.reshape(n, cap)
    high = jnp.where(is_live, slots // LANES, -1).astype(F32)
    low = (slots % LANES).astype(F32)

    positions = jnp.arange(list_width)
    discount = 1.0 / jnp.log2(2.0 + positions.astype(F32))
    weights = jnp.abs(discount[:, None] - discount[None, :]).reshape(per_list, LANES, list_width)
    keep = positions[None, :] < list_lengths[:, None]
    gain_rows = jnp.where(keep, gains, 0.0).reshape(high_rows, LANES)
    keep_rows = keep.astype(F32).reshape(high_rows, LANES)

    wo_top = lax.reduce_precision(weight_out, exponent_bits=8, mantissa_bits=7)
    wo_rest = (weight_out - wo_top).astype(BF)
    wo_top = wo_top.astype(BF)
    lane = jnp.arange(LANES)[None, :]
    wo_pair = jnp.where(
        lane == 0, wo_top[:, None], jnp.where(lane == 1, wo_rest[:, None], jnp.zeros((), BF))
    )

    hid, slope, scores = forward(
        log_rows, weight_in.astype(BF), bias_in.reshape(1, hidden), wo_pair
    )
    message = jnp.stack([scores.reshape(n, cap), high, low], axis=1)
    doc_rows, lam = middle(n, message, gain_rows, keep_rows, weights, list_count * n)
    lambdas = doc_rows.reshape(list_count, list_width)

    spans = hidden // LANES
    row_parts = max(1, n // spans)
    unit = 16 * row_parts
    padded = (features + 16 + unit - 1) // unit * unit
    parts = backward(
        log_rows, hid, slope, lam.reshape(total // BLOCK, 1, BLOCK),
        weight_out.reshape(1, hidden), padded,
    )
    grads = sum_over_dp(n, parts.reshape(n, padded * spans // n, LANES))
    grads = grads.reshape(spans, padded, LANES)
    grad_b = grads[:, features, :].reshape(hidden).astype(F32)
    grad_o = grads[:, features + 1, :].reshape(hidden).astype(F32)
    return (
        lambdas,
        *adam_matrix(grads, weight_in, moment_w, second_w),
        *adam_step(bias_in, moment_b, second_b, grad_b),
        *adam_step(weight_out, moment_o, second_o, grad_o),
    )


def solution(mesh):
    dp, mp, both = P("dp"), P("mp"), P(None, "mp")
    rows = P("dp", None)
    return jax.shard_map(
        per_device,
        mesh=mesh,
        in_specs=(rows, dp, dp, rows, dp, rows, both, mp, mp, both, both, mp, mp, mp, mp),
        out_specs=(rows, both, both, both, mp, mp, mp, mp, mp, mp),
        check_vma=False,
    )
```

```python
import functools
import math

import jax
import jax.numpy as jnp
from jax import lax
from jax.experimental import pallas as pl
from jax.experimental.pallas import tpu as pltpu
from jax.sharding import PartitionSpec as P

beta_one = 0.9
beta_two = 0.95
learn_rate = 0.001
adam_eps = 1e-08

C0 = math.sqrt(2.0 / math.pi)
C1 = C0 * 0.044715
MESH = pl.DeviceIdType.MESH
LANES = 128
BLOCK = 512
WIDE = 256
BF = jnp.bfloat16
F32 = jnp.float32


def fwd_kernel(x_ref, w_ref, b_ref, wo_ref, h_ref, g_ref, s_ref, w_low):
    @pl.when(pl.program_id(0) == 0)
    def _():
        w_low[...] = w_ref[...].astype(BF)

    x = x_ref[...]
    acc = jnp.zeros((x.shape[0], LANES), F32)
    for k in range(h_ref.shape[0]):
        cols = slice(k * WIDE, (k + 1) * WIDE)
        v = jnp.dot(x, w_low[:, cols], preferred_element_type=F32) + b_ref[:, cols]
        v2 = v * v
        t = jnp.tanh(v * (C1 * v2 + C0))
        up = 1.0 + t
        h = v * up
        g = up + (h * (1.0 - t)) * ((3.0 * C1) * v2 + C0)
        hb = h.astype(BF)
        h_ref[k] = hb
        g_ref[k] = g.astype(BF)
        acc = acc + jnp.dot(hb, wo_ref[cols, :], preferred_element_type=F32)
    s_ref[0] = jnp.sum(acc.T, axis=0, keepdims=True)


def forward(rows, weights, bias, wo_pair):
    total, features = rows.shape
    hidden = weights.shape[1]
    blocks = total // BLOCK
    groups = hidden // WIDE
    return pl.pallas_call(
        fwd_kernel,
        grid=(blocks,),
        in_specs=[
            pl.BlockSpec((BLOCK, features), lambda i: (i, 0)),
            pl.BlockSpec((features, hidden), lambda i: (0, 0)),
            pl.BlockSpec((1, hidden), lambda i: (0, 0)),
            pl.BlockSpec((hidden, LANES), lambda i: (0, 0)),
        ],
        out_specs=[
            pl.BlockSpec((groups, BLOCK, WIDE), lambda i: (0, i, 0)),
            pl.BlockSpec((groups, BLOCK, WIDE), lambda i: (0, i, 0)),
            pl.BlockSpec((1, 1, BLOCK), lambda i: (i, 0, 0)),
        ],
        out_shape=[
            jax.ShapeDtypeStruct((groups, total, WIDE), BF),
            jax.ShapeDtypeStruct((groups, total, WIDE), BF),
            jax.ShapeDtypeStruct((blocks, 1, BLOCK), F32),
        ],
        scratch_shapes=[pltpu.VMEM((features, hidden), BF)],
        compiler_params=pltpu.CompilerParams(vmem_limit_bytes=48 << 20),
    )(rows, weights, bias, wo_pair)


def split_three(values):
    first = values.astype(BF)
    rest = values - first.astype(F32)
    second = rest.astype(BF)
    third = (rest - second.astype(F32)).astype(BF)
    return first, second, third


def mid_kernel(
    n, cores, scale, msg_ref, gain_ref, keep_ref, weight_ref,
    doc_ref, lam_ref,
    arrive, lam_out, lam_in, s_row, l_row, s_col, g_col, lam_t,
    send_a, recv_a, send_l, recv_l,
):
    me = lax.axis_index("dp")
    core = lax.axis_index("mp")
    high_rows = gain_ref.shape[0]
    per_list = weight_ref.shape[0]
    lists = high_rows // per_list
    cap = msg_ref.shape[2]

    barrier = pltpu.get_barrier_semaphore()

    @pl.loop(1, n)
    def _(k):
        peer = lax.rem(me + k, n)
        for d in range(cores):
            pl.semaphore_signal(
                barrier, inc=1, device_id=(peer, lax.rem(core + d, cores)), device_id_type=MESH
            )

    for d in range(1, cores):
        pl.semaphore_signal(
            barrier, inc=1, device_id=(me, lax.rem(core + d, cores)), device_id_type=MESH
        )
    pl.semaphore_wait(barrier, cores * n - 1)

    def score_copy(peer, d):
        return pltpu.make_async_remote_copy(
            src_ref=msg_ref.at[peer],
            dst_ref=arrive.at[core, me],
            send_sem=send_a.at[d, peer],
            recv_sem=recv_a.at[core, me],
            device_id=(peer, lax.rem(core + d, cores)),
            device_id_type=MESH,
        )

    def arrival(from_core, peer):
        return pltpu.make_async_remote_copy(
            src_ref=msg_ref.at[peer],
            dst_ref=arrive.at[from_core, peer],
            send_sem=send_a.at[0, peer],
            recv_sem=recv_a.at[from_core, peer],
            device_id=(peer, from_core),
            device_id_type=MESH,
        )

    @pl.loop(1, n)
    def _(k):
        peer = lax.rem(me + k, n)
        for d in range(cores):
            score_copy(peer, d).start()

    for d in range(1, cores):
        score_copy(me, d).start()
    arrive[core, me] = msg_ref[me]

    high_iota = lax.broadcasted_iota(jnp.int32, (LANES, cap), 0).astype(F32)

    def absorb(shard, total):
        first = arrive[0, shard]
        value = first[0:1]
        for c in range(1, cores):
            value = value + arrive[c, shard][0:1]
        low = (first[2:3] == high_iota).astype(F32).astype(BF)
        at_high = first[1:2] == high_iota[:high_rows]
        spread = jnp.concatenate(
            [jnp.where(at_high, piece.astype(F32), 0.0).astype(BF) for piece in split_three(value)],
            axis=0,
        )
        sums = lax.dot_general(
            spread, low, (((1,), (1,)), ((), ())), preferred_element_type=F32
        )
        return total + (
            sums[:high_rows] + sums[high_rows : 2 * high_rows] + sums[2 * high_rows :]
        )

    for d in range(1, cores):
        arrival(lax.rem(core + d, cores), me).wait_recv()
    total = absorb(me, jnp.zeros((high_rows, LANES), F32))

    def take(k, total):
        for j in range(3):
            for c in range(cores):
                arrival(c, lax.rem(me + 1 + 3 * k + j, n)).wait_recv()
        for j in range(3):
            total = absorb(lax.rem(me + 1 + 3 * k + j, n), total)
        return total

    total = lax.fori_loop(0, (n - 1) // 3, take, total)
    scores = jnp.where(keep_ref[...] > 0.0, 0.5 * total, -1e30)
    s_row[...] = scores
    padding = jnp.zeros((LANES - high_rows, LANES), F32)
    s_turn = jnp.concatenate([scores, padding], axis=0).T
    g_turn = jnp.concatenate([gain_ref[...], padding], axis=0).T
    for i in range(high_rows):
        s_col[i] = s_turn[:, i : i + 1]
        g_col[i] = g_turn[:, i : i + 1]

    def one_list(q, carry):
        base = q * per_list
        row_s = jnp.concatenate([s_row[pl.ds(base + k, 1), :] for k in range(per_list)], axis=1)
        row_g = jnp.concatenate([gain_ref[pl.ds(base + k, 1), :] for k in range(per_list)], axis=1)
        sums = jnp.zeros((8, row_s.shape[1]), F32)
        for k in range(per_list):
            col_s = s_col[base + k]
            col_g = g_col[base + k]
            for r in range(0, LANES, 8):
                delta_g = col_g[r : r + 8] - row_g
                delta_t = jnp.tanh(col_s[r : r + 8] - row_s)
                sums = sums + weight_ref[k, r : r + 8, :] * (delta_g - jnp.abs(delta_g) * delta_t)
        lam = 0.5 * jnp.sum(sums, axis=0, keepdims=True)
        for k in range(per_list):
            l_row[pl.ds(base + k, 1), :] = lam[:, k * LANES : (k + 1) * LANES]
        return carry

    lax.fori_loop(0, lists, one_list, 0)
    doc_ref[...] = l_row[...]
    turned = jnp.concatenate([l_row[...] * scale, padding], axis=0).T
    lam_t[...] = jnp.concatenate(split_three(turned), axis=1)

    def answer(shard):
        info = arrive[core, shard]
        low = info[2:3] == high_iota
        high = (info[1:2] == high_iota).astype(F32).astype(BF)
        spread = jnp.dot(
            lam_t[...], jnp.concatenate([high] * 3, axis=0), preferred_element_type=F32
        )
        return jnp.sum(jnp.where(low, spread, 0.0), axis=0, keepdims=True)

    def lam_copy(peer):
        return pltpu.make_async_remote_copy(
            src_ref=lam_out.at[peer],
            dst_ref=lam_in.at[me],
            send_sem=send_l.at[peer],
            recv_sem=recv_l.at[me],
            device_id=(peer, core),
            device_id_type=MESH,
        )

    def lam_arrival(peer):
        return pltpu.make_async_remote_copy(
            src_ref=lam_out.at[peer],
            dst_ref=lam_in.at[peer],
            send_sem=send_l.at[peer],
            recv_sem=recv_l.at[peer],
            device_id=(peer, core),
            device_id_type=MESH,
        )

    @pl.loop(0, (n - 1) // 3)
    def _(k):
        peers = [lax.rem(me + 1 + 3 * k + j, n) for j in range(3)]
        replies = [answer(peer) for peer in peers]
        for peer, reply in zip(peers, replies):
            lam_out[peer] = reply
        for peer in peers:
            lam_copy(peer).start()

    lam_ref[me] = answer(me)

    @pl.loop(1, n)
    def _(k):
        peer = lax.rem(me + k, n)
        lam_arrival(peer).wait_recv()
        lam_ref[peer] = lam_in[peer]

    @pl.loop(1, n)
    def _(k):
        peer = lax.rem(me + k, n)
        for d in range(cores):
            score_copy(peer, d).wait_send()
        lam_copy(peer).wait_send()

    for d in range(1, cores):
        score_copy(me, d).wait_send()


def middle(n, cores, message, gain_rows, keep_rows, weights, query_total):
    cap = message.shape[2]
    high_rows = gain_rows.shape[0]
    vmem = pl.BlockSpec(memory_space=pltpu.VMEM)
    return pl.pallas_call(
        functools.partial(mid_kernel, n, cores, 1.0 / query_total),
        in_specs=[vmem] * 4,
        out_specs=[vmem] * 2,
        out_shape=[
            jax.ShapeDtypeStruct((high_rows, LANES), F32),
            jax.ShapeDtypeStruct((n, 1, cap), F32),
        ],
        scratch_shapes=[
            pltpu.VMEM((cores, n, 3, cap), F32),
            pltpu.VMEM((n, 1, cap), F32),
            pltpu.VMEM((n, 1, cap), F32),
            pltpu.VMEM((high_rows, LANES), F32),
            pltpu.VMEM((high_rows, LANES), F32),
            pltpu.VMEM((high_rows, LANES, 1), F32),
            pltpu.VMEM((high_rows, LANES, 1), F32),
            pltpu.VMEM((LANES, 3 * LANES), BF),
            pltpu.SemaphoreType.DMA((cores, n)),
            pltpu.SemaphoreType.DMA((cores, n)),
            pltpu.SemaphoreType.DMA((n,)),
            pltpu.SemaphoreType.DMA((n,)),
        ],
        compiler_params=pltpu.CompilerParams(
            collective_id=0, has_side_effects=True, vmem_limit_bytes=48 << 20
        ),
    )(message, gain_rows, keep_rows, weights)


def tail_rows(grad_b, grad_o):
    spot = lax.broadcasted_iota(jnp.int32, (16, grad_b.shape[1]), 0)
    top_b = grad_b.astype(BF).astype(F32)
    top_o = grad_o.astype(BF).astype(F32)
    tail = jnp.where(spot == 0, top_b, jnp.where(spot == 1, top_o, 0.0))
    tail = jnp.where(spot == 2, grad_b - top_b, jnp.where(spot == 3, grad_o - top_o, tail))
    return tail.astype(BF)


def grad_kernel(
    n, parts_per_span, x_ref, lam_ref, wo_ref, h_hbm, g_hbm, out_ref,
    left, h_buf, g_buf, parts, arrive, mine, full,
    fetch_sem, send_a, recv_a, send_b, recv_b,
):
    me = lax.axis_index("dp")
    core = lax.axis_index("mp")
    groups = h_hbm.shape[0]
    features = x_ref.shape[1]
    chunk_rows = parts.shape[1]
    padded = chunk_rows * parts_per_span
    per_group = WIDE // LANES * parts_per_span
    first = me // per_group + 1

    def fetches(k):
        group = lax.rem(first + k, groups)
        slot = lax.rem(k, 2)
        return (
            pltpu.make_async_copy(g_hbm.at[group], g_buf.at[slot], fetch_sem.at[slot, 0]),
            pltpu.make_async_copy(h_hbm.at[group], h_buf.at[slot], fetch_sem.at[slot, 1]),
        )

    for one in fetches(0):
        one.start()

    barrier = pltpu.get_barrier_semaphore()

    @pl.loop(1, n)
    def _(k):
        peer = lax.rem(me + k, n)
        pl.semaphore_signal(barrier, inc=1, device_id=(peer, core), device_id_type=MESH)

    @pl.loop(0, lam_ref.shape[0])
    def _(i):
        lam = lam_ref[i]
        top = lam.astype(BF).astype(F32)
        place = lax.broadcasted_iota(jnp.int32, (16, BLOCK), 0)
        pair = jnp.where(place == 0, top, jnp.where(place == 1, lam - top, 0.0)).astype(BF)
        at = pl.ds(pl.multiple_of(i * BLOCK, BLOCK), BLOCK)
        left[:features, at] = (x_ref[at, :].astype(F32).T * lam).astype(BF)
        left[features:, at] = pair

    pl.semaphore_wait(barrier, n - 1)

    def copy(source, target, send, recvs, peer, slot):
        return pltpu.make_async_remote_copy(
            src_ref=source,
            dst_ref=target.at[slot],
            send_sem=send,
            recv_sem=recvs.at[slot],
            device_id=(peer, core),
            device_id_type=MESH,
        )

    @pl.loop(0, groups)
    def _(k):
        for one in fetches(k):
            one.wait()

        @pl.when(k + 1 < groups)
        def _():
            for one in fetches(k + 1):
                one.start()

        group = lax.rem(first + k, groups)
        slot = lax.rem(k, 2)
        half_wo = wo_ref[group]
        sums = jnp.dot(left[...], g_buf[slot], preferred_element_type=F32)
        sums_o = jnp.dot(left[features:, :], h_buf[slot], preferred_element_type=F32)
        grad_b = jnp.sum(sums[features:], axis=0, keepdims=True) * half_wo
        grad_o = 0.5 * jnp.sum(sums_o, axis=0, keepdims=True)
        pieces = [
            (sums[:features] * half_wo).astype(BF),
            tail_rows(grad_b, grad_o),
        ]
        if padded > features + 16:
            pieces.append(jnp.zeros((padded - features - 16, WIDE), BF))
        block = jnp.concatenate(pieces, axis=0)
        for j in range(per_group):
            span, part = j // parts_per_span, j % parts_per_span
            parts[group * per_group + j] = block[
                part * chunk_rows : (part + 1) * chunk_rows, span * LANES : (span + 1) * LANES
            ]
        for j in range(per_group):
            owner = group * per_group + j

            @pl.when(owner != me)
            def _():
                copy(parts.at[owner], arrive, send_a.at[owner], recv_a, owner, me).start()

    def take(k, total):
        peer = lax.rem(me + n - k, n)
        copy(parts.at[peer], arrive, send_a.at[peer], recv_a, peer, peer).wait_recv()
        return total + arrive[peer].astype(F32)

    total = lax.fori_loop(1, n, take, parts[me].astype(F32))
    mine[...] = total.astype(BF)

    @pl.when(lax.rem(me, parts_per_span) == features // chunk_rows)
    def _():
        at = features % chunk_rows
        mine[at : at + 16, :] = tail_rows(
            total[at : at + 1] + total[at + 2 : at + 3],
            total[at + 1 : at + 2] + total[at + 3 : at + 4],
        )

    inner = 4
    outer = n // inner
    row, col = me // inner, lax.rem(me, inner)

    def outer_peer(i):
        return lax.rem(row + i, outer) * inner + col

    def inner_peer(j):
        return row * inner + lax.rem(col + j, inner)

    def send_outer(i):
        peer = outer_peer(i)
        return copy(mine, full, send_b.at[0, peer], recv_b, peer, me)

    def send_inner(j):
        return copy(mine, full, send_b.at[j, me], recv_b, inner_peer(j), me)

    def pass_on(i, j):
        chunk = outer_peer(outer - i)
        return copy(full.at[chunk], full, send_b.at[j, chunk], recv_b, inner_peer(j), chunk)

    def landed(chunk):
        return copy(mine, full, send_b.at[0, chunk], recv_b, me, chunk)

    for i in range(1, outer):
        send_outer(i).start()
    for j in range(1, inner):
        send_inner(j).start()
    out_ref[me] = mine[...]
    for i in range(1, outer):
        chunk = outer_peer(outer - i)
        landed(chunk).wait_recv()
        for j in range(1, inner):
            pass_on(i, j).start()
        out_ref[chunk] = full[chunk]
    for i in range(outer):
        for j in range(1, inner):
            chunk = lax.rem(row + outer - i, outer) * inner + lax.rem(col + j, inner)
            landed(chunk).wait_recv()
            out_ref[chunk] = full[chunk]

    @pl.loop(1, n)
    def _(k):
        peer = lax.rem(me + k, n)
        copy(parts.at[peer], arrive, send_a.at[peer], recv_a, peer, me).wait_send()

    for i in range(1, outer):
        send_outer(i).wait_send()
        for j in range(1, inner):
            pass_on(i, j).wait_send()
    for j in range(1, inner):
        send_inner(j).wait_send()


def gradients(n, rows, hid, slope, lam, wo_half, parts_per_span, chunk_rows):
    total, features = rows.shape
    groups = hid.shape[0]
    vmem = pl.BlockSpec(memory_space=pltpu.VMEM)
    hbm = pl.BlockSpec(memory_space=pl.ANY)
    shape = (n, chunk_rows, LANES)
    return pl.pallas_call(
        functools.partial(grad_kernel, n, parts_per_span),
        in_specs=[vmem, vmem, vmem, hbm, hbm],
        out_specs=vmem,
        out_shape=jax.ShapeDtypeStruct(shape, BF),
        scratch_shapes=[
            pltpu.VMEM((features + 16, total), BF),
            pltpu.VMEM((2, total, WIDE), BF),
            pltpu.VMEM((2, total, WIDE), BF),
            pltpu.VMEM(shape, BF),
            pltpu.VMEM(shape, BF),
            pltpu.VMEM(shape[1:], BF),
            pltpu.VMEM(shape, BF),
            pltpu.SemaphoreType.DMA((2, 2)),
            pltpu.SemaphoreType.DMA((n,)),
            pltpu.SemaphoreType.DMA((n,)),
            pltpu.SemaphoreType.DMA((4, n)),
            pltpu.SemaphoreType.DMA((n,)),
        ],
        compiler_params=pltpu.CompilerParams(
            collective_id=1, has_side_effects=True, vmem_limit_bytes=48 << 20
        ),
    )(rows, lam, wo_half, hid, slope)


def adam_step(weights, moment, second, gradient):
    moment_next = beta_one * moment + (1.0 - beta_one) * gradient
    second_next = beta_two * second + (1.0 - beta_two) * gradient * gradient
    weights_next = weights - learn_rate * moment_next / (jnp.sqrt(second_next) + adam_eps)
    return (weights_next, moment_next, second_next)


def adam_kernel(g_ref, w_ref, m_ref, s_ref, w_out, m_out, s_out):
    features = w_ref.shape[0]
    for k in range(g_ref.shape[0]):
        cols = slice(k * LANES, (k + 1) * LANES)
        grad = g_ref[k, :features, :].astype(F32)
        w_out[:, cols], m_out[:, cols], s_out[:, cols] = adam_step(
            w_ref[:, cols], m_ref[:, cols], s_ref[:, cols], grad
        )


def adam_matrix(grads, weights, moment, second):
    features, hidden = weights.shape
    group = 4
    block = pl.BlockSpec((features, group * LANES), lambda i: (0, i))
    return pl.pallas_call(
        adam_kernel,
        grid=(hidden // (group * LANES),),
        in_specs=[pl.BlockSpec((group,) + grads.shape[1:], lambda i: (i, 0, 0))] + [block] * 3,
        out_specs=[block] * 3,
        out_shape=[jax.ShapeDtypeStruct(weights.shape, F32)] * 3,
    )(grads, weights, moment, second)


def per_device(
    log_rows, query_ids, doc_ranks, row_counts, list_lengths, gains,
    weight_in, bias_in, weight_out, moment_w, second_w,
    moment_b, second_b, moment_o, second_o,
):
    n = lax.axis_size("dp")
    total, features = log_rows.shape
    cap = total // n
    hidden = weight_in.shape[1]
    list_count, list_width = gains.shape
    high_rows = list_count * list_width // LANES
    per_list = list_width // LANES

    is_live = jnp.arange(cap)[None, :] < row_counts.reshape(n, 1)
    slots = query_ids.reshape(n, cap) % list_count * list_width + doc_ranks.reshape(n, cap)
    high = jnp.where(is_live, slots // LANES, -1).astype(F32)
    low = (slots % LANES).astype(F32)

    positions = jnp.arange(list_width)
    discount = 1.0 / jnp.log2(2.0 + positions.astype(F32))
    weights = jnp.abs(discount[:, None] - discount[None, :]).reshape(per_list, LANES, list_width)
    keep = positions[None, :] < list_lengths[:, None]
    gain_rows = jnp.where(keep, gains, 0.0).reshape(high_rows, LANES)
    keep_rows = keep.astype(F32).reshape(high_rows, LANES)

    wo_half = 0.5 * weight_out
    wo_top = lax.reduce_precision(wo_half, exponent_bits=8, mantissa_bits=7)
    wo_rest = (wo_half - wo_top).astype(BF)
    wo_top = wo_top.astype(BF)
    lane = jnp.arange(LANES)[None, :]
    wo_pair = jnp.where(
        lane == 0, wo_top[:, None], jnp.where(lane == 1, wo_rest[:, None], jnp.zeros((), BF))
    )

    hid, slope, scores = forward(log_rows, weight_in, bias_in.reshape(1, hidden), wo_pair)
    message = jnp.stack([scores.reshape(n, cap), high, low], axis=1)
    doc_rows, lam = middle(
        n, lax.axis_size("mp"), message, gain_rows, keep_rows, weights, list_count * n
    )
    lambdas = doc_rows.reshape(list_count, list_width)

    spans = hidden // LANES
    row_parts = max(1, n // spans)
    unit = 16 * row_parts
    padded = (features + 16 + unit - 1) // unit * unit
    grads = gradients(
        n, log_rows, hid, slope, lam.reshape(total // BLOCK, 1, BLOCK),
        wo_half.reshape(hidden // WIDE, 1, WIDE), row_parts, padded // row_parts,
    )
    grads = grads.reshape(spans, padded, LANES)
    tail = grads[:, features : features + 4, :].astype(F32)
    grad_b = (tail[:, 0] + tail[:, 2]).reshape(hidden)
    grad_o = (tail[:, 1] + tail[:, 3]).reshape(hidden)
    return (
        lambdas,
        *adam_matrix(grads, weight_in, moment_w, second_w),
        *adam_step(bias_in, moment_b, second_b, grad_b),
        *adam_step(weight_out, moment_o, second_o, grad_o),
    )


def solution(mesh):
    dp, mp, both = P("dp"), P("mp"), P(None, "mp")
    rows = P("dp", None)
    return jax.shard_map(
        per_device,
        mesh=mesh,
        in_specs=(rows, dp, dp, rows, dp, rows, both, mp, mp, both, both, mp, mp, mp, mp),
        out_specs=(rows, both, both, both, mp, mp, mp, mp, mp, mp),
        check_vma=False,
    )
```

```python
import functools
import math

import jax
import jax.numpy as jnp
from jax import lax
from jax.experimental import pallas as pl
from jax.experimental.pallas import tpu as pltpu
from jax.sharding import PartitionSpec as P

beta_one = 0.9
beta_two = 0.95
learn_rate = 0.001
adam_eps = 1e-08

C0 = math.sqrt(2.0 / math.pi)
C1 = C0 * 0.044715
MESH = pl.DeviceIdType.MESH
LANES = 128
BLOCK = 512
WIDE = 256
BF = jnp.bfloat16
F32 = jnp.float32


def split_three(values):
    first = values.astype(BF)
    rest = values - first.astype(F32)
    second = rest.astype(BF)
    third = (rest - second.astype(F32)).astype(BF)
    return first, second, third


def score_kernel(
    n, cores, scale, x_ref, w_ref, b_ref, wo_ref, slot_ref, gain_ref, keep_ref, weight_ref,
    h_ref, g_ref, doc_ref, lam_ref,
    w_low, msg_ref, arrive, lam_out, lam_in, s_row, l_row, s_col, g_col, lam_t,
    send_a, recv_a, send_l, recv_l,
):
    me = lax.axis_index("dp")
    core = lax.axis_index("mp")
    high_rows = gain_ref.shape[0]
    per_list = weight_ref.shape[0]
    lists = high_rows // per_list
    cap = msg_ref.shape[2]
    step = pl.program_id(0)
    barrier = pltpu.get_barrier_semaphore()

    @pl.when(step == 0)
    def _():
        @pl.loop(1, n)
        def _(k):
            peer = lax.rem(me + k, n)
            for d in range(cores):
                pl.semaphore_signal(
                    barrier, inc=1, device_id=(peer, lax.rem(core + d, cores)), device_id_type=MESH
                )

        for d in range(1, cores):
            pl.semaphore_signal(
                barrier, inc=1, device_id=(me, lax.rem(core + d, cores)), device_id_type=MESH
            )
        w_low[...] = w_ref[...].astype(BF)

    x = x_ref[...]
    acc = jnp.zeros((cap, LANES), F32)
    for k in range(h_ref.shape[0]):
        cols = slice(k * WIDE, (k + 1) * WIDE)
        v = jnp.dot(x, w_low[:, cols], preferred_element_type=F32) + b_ref[:, cols]
        v2 = v * v
        t = jnp.tanh(v * (C1 * v2 + C0))
        up = 1.0 + t
        h = v * up
        g = up + (h * (1.0 - t)) * ((3.0 * C1) * v2 + C0)
        hb = h.astype(BF)
        h_ref[k] = hb
        g_ref[k] = g.astype(BF)
        acc = acc + jnp.dot(hb, wo_ref[cols, :], preferred_element_type=F32)
    msg_ref[step, 0:1, :] = jnp.sum(acc.T, axis=0, keepdims=True)
    msg_ref[step, 1:3, :] = slot_ref[0]

    @pl.when(step == 0)
    def _():
        pl.semaphore_wait(barrier, cores * n - 1)

    def score_copy(peer, d):
        return pltpu.make_async_remote_copy(
            src_ref=msg_ref.at[peer],
            dst_ref=arrive.at[core, me],
            send_sem=send_a.at[d, peer],
            recv_sem=recv_a.at[core, me],
            device_id=(peer, lax.rem(core + d, cores)),
            device_id_type=MESH,
        )

    def arrival(from_core, peer):
        return pltpu.make_async_remote_copy(
            src_ref=msg_ref.at[peer],
            dst_ref=arrive.at[from_core, peer],
            send_sem=send_a.at[0, peer],
            recv_sem=recv_a.at[from_core, peer],
            device_id=(peer, from_core),
            device_id_type=MESH,
        )

    def finish():
        arrive[core, me] = msg_ref[me]
        high_iota = lax.broadcasted_iota(jnp.int32, (LANES, cap), 0).astype(F32)

        def absorb(shard, total):
            first = arrive[0, shard]
            value = first[0:1]
            for c in range(1, cores):
                value = value + arrive[c, shard][0:1]
            low = (first[2:3] == high_iota).astype(F32).astype(BF)
            at_high = first[1:2] == high_iota[:high_rows]
            spread = jnp.concatenate(
                [jnp.where(at_high, piece.astype(F32), 0.0).astype(BF) for piece in split_three(value)],
                axis=0,
            )
            sums = lax.dot_general(
                spread, low, (((1,), (1,)), ((), ())), preferred_element_type=F32
            )
            return total + (
                sums[:high_rows] + sums[high_rows : 2 * high_rows] + sums[2 * high_rows :]
            )

        for d in range(1, cores):
            arrival(lax.rem(core + d, cores), me).wait_recv()
        total = absorb(me, jnp.zeros((high_rows, LANES), F32))

        def take(k, total):
            for j in range(3):
                for c in range(cores):
                    arrival(c, lax.rem(me + 1 + 3 * k + j, n)).wait_recv()
            for j in range(3):
                total = absorb(lax.rem(me + 1 + 3 * k + j, n), total)
            return total

        total = lax.fori_loop(0, (n - 1) // 3, take, total)
        scores = jnp.where(keep_ref[...] > 0.0, 0.5 * total, -1e30)
        s_row[...] = scores
        padding = jnp.zeros((LANES - high_rows, LANES), F32)
        s_turn = jnp.concatenate([scores, padding], axis=0).T
        g_turn = jnp.concatenate([gain_ref[...], padding], axis=0).T
        for i in range(high_rows):
            s_col[i] = s_turn[:, i : i + 1]
            g_col[i] = g_turn[:, i : i + 1]

        def one_list(q, carry):
            base = q * per_list
            row_s = jnp.concatenate([s_row[pl.ds(base + k, 1), :] for k in range(per_list)], axis=1)
            row_g = jnp.concatenate([gain_ref[pl.ds(base + k, 1), :] for k in range(per_list)], axis=1)
            sums = jnp.zeros((8, row_s.shape[1]), F32)
            for k in range(per_list):
                col_s = s_col[base + k]
                col_g = g_col[base + k]
                for r in range(0, LANES, 8):
                    delta_g = col_g[r : r + 8] - row_g
                    delta_t = jnp.tanh(col_s[r : r + 8] - row_s)
                    sums = sums + weight_ref[k, r : r + 8, :] * (delta_g - jnp.abs(delta_g) * delta_t)
            lam = 0.5 * jnp.sum(sums, axis=0, keepdims=True)
            for k in range(per_list):
                l_row[pl.ds(base + k, 1), :] = lam[:, k * LANES : (k + 1) * LANES]
            return carry

        lax.fori_loop(0, lists, one_list, 0)
        doc_ref[...] = l_row[...]
        turned = jnp.concatenate([l_row[...] * scale, padding], axis=0).T
        lam_t[...] = jnp.concatenate(split_three(turned), axis=1)

        def answer(shard):
            info = arrive[core, shard]
            low = info[2:3] == high_iota
            high = (info[1:2] == high_iota).astype(F32).astype(BF)
            spread = jnp.dot(
                lam_t[...], jnp.concatenate([high] * 3, axis=0), preferred_element_type=F32
            )
            return jnp.sum(jnp.where(low, spread, 0.0), axis=0, keepdims=True)

        def lam_copy(peer):
            return pltpu.make_async_remote_copy(
                src_ref=lam_out.at[peer],
                dst_ref=lam_in.at[me],
                send_sem=send_l.at[peer],
                recv_sem=recv_l.at[me],
                device_id=(peer, core),
                device_id_type=MESH,
            )

        def lam_arrival(peer):
            return pltpu.make_async_remote_copy(
                src_ref=lam_out.at[peer],
                dst_ref=lam_in.at[peer],
                send_sem=send_l.at[peer],
                recv_sem=recv_l.at[peer],
                device_id=(peer, core),
                device_id_type=MESH,
            )

        @pl.loop(0, (n - 1) // 3)
        def _(k):
            peers = [lax.rem(me + 1 + 3 * k + j, n) for j in range(3)]
            replies = [answer(peer) for peer in peers]
            for peer, reply in zip(peers, replies):
                lam_out[peer] = reply
            for peer in peers:
                lam_copy(peer).start()

        lam_ref[me] = answer(me)

        @pl.loop(1, n)
        def _(k):
            peer = lax.rem(me + k, n)
            lam_arrival(peer).wait_recv()
            lam_ref[peer] = lam_in[peer]

        @pl.loop(1, n)
        def _(k):
            peer = lax.rem(me + k, n)
            for d in range(cores):
                score_copy(peer, d).wait_send()
            lam_copy(peer).wait_send()

        for d in range(1, cores):
            score_copy(me, d).wait_send()

    for d in range(1, cores):
        score_copy(step, d).start()

    @pl.when(step != me)
    def _():
        score_copy(step, 0).start()

    pl.when(step == n - 1)(finish)


def score(n, cores, rows, weights, bias, wo_pair, slots, gain_rows, keep_rows, pair_weights, total_lists):
    total, features = rows.shape
    hidden = weights.shape[1]
    groups = hidden // WIDE
    cap = total // n
    high_rows = gain_rows.shape[0]

    def whole(array):
        return pl.BlockSpec(array.shape, lambda i: (0,) * array.ndim)

    block = pl.BlockSpec((groups, cap, WIDE), lambda i: (0, i, 0))
    kept = jax.ShapeDtypeStruct((groups, total, WIDE), BF)
    return pl.pallas_call(
        functools.partial(score_kernel, n, cores, 1.0 / total_lists),
        grid=(n,),
        in_specs=[
            pl.BlockSpec((cap, features), lambda i: (i, 0)),
            whole(weights), whole(bias), whole(wo_pair),
            pl.BlockSpec((1, 2, cap), lambda i: (i, 0, 0)),
            whole(gain_rows), whole(keep_rows), whole(pair_weights),
        ],
        out_specs=[
            block, block,
            pl.BlockSpec((high_rows, LANES), lambda i: (0, 0)),
            pl.BlockSpec((n, 1, cap), lambda i: (0, 0, 0)),
        ],
        out_shape=[
            kept, kept,
            jax.ShapeDtypeStruct((high_rows, LANES), F32),
            jax.ShapeDtypeStruct((n, 1, cap), F32),
        ],
        scratch_shapes=[
            pltpu.VMEM((features, hidden), BF),
            pltpu.VMEM((n, 3, cap), F32),
            pltpu.VMEM((cores, n, 3, cap), F32),
            pltpu.VMEM((n, 1, cap), F32),
            pltpu.VMEM((n, 1, cap), F32),
            pltpu.VMEM((high_rows, LANES), F32),
            pltpu.VMEM((high_rows, LANES), F32),
            pltpu.VMEM((high_rows, LANES, 1), F32),
            pltpu.VMEM((high_rows, LANES, 1), F32),
            pltpu.VMEM((LANES, 3 * LANES), BF),
            pltpu.SemaphoreType.DMA((cores, n)),
            pltpu.SemaphoreType.DMA((cores, n)),
            pltpu.SemaphoreType.DMA((n,)),
            pltpu.SemaphoreType.DMA((n,)),
        ],
        compiler_params=pltpu.CompilerParams(
            collective_id=0, has_side_effects=True, vmem_limit_bytes=48 << 20
        ),
    )(rows, weights, bias, wo_pair, slots, gain_rows, keep_rows, pair_weights)


def tail_rows(grad_b, grad_o):
    spot = lax.broadcasted_iota(jnp.int32, (16, grad_b.shape[1]), 0)
    top_b = grad_b.astype(BF).astype(F32)
    top_o = grad_o.astype(BF).astype(F32)
    tail = jnp.where(spot == 0, top_b, jnp.where(spot == 1, top_o, 0.0))
    tail = jnp.where(spot == 2, grad_b - top_b, jnp.where(spot == 3, grad_o - top_o, tail))
    return tail.astype(BF)


def grad_kernel(
    n, parts_per_span, x_ref, lam_ref, wo_ref, h_hbm, g_hbm, out_ref,
    left, h_buf, g_buf, parts, arrive, mine, full,
    fetch_sem, send_a, recv_a, send_b, recv_b,
):
    me = lax.axis_index("dp")
    core = lax.axis_index("mp")
    groups = h_hbm.shape[0]
    features = x_ref.shape[1]
    chunk_rows = parts.shape[1]
    padded = chunk_rows * parts_per_span
    per_group = WIDE // LANES * parts_per_span
    first = me // per_group + 1

    def fetches(k):
        group = lax.rem(first + k, groups)
        slot = lax.rem(k, 2)
        return (
            pltpu.make_async_copy(g_hbm.at[group], g_buf.at[slot], fetch_sem.at[slot, 0]),
            pltpu.make_async_copy(h_hbm.at[group], h_buf.at[slot], fetch_sem.at[slot, 1]),
        )

    for one in fetches(0):
        one.start()

    barrier = pltpu.get_barrier_semaphore()

    @pl.loop(1, n)
    def _(k):
        peer = lax.rem(me + k, n)
        pl.semaphore_signal(barrier, inc=1, device_id=(peer, core), device_id_type=MESH)

    @pl.loop(0, lam_ref.shape[0])
    def _(i):
        lam = lam_ref[i]
        top = lam.astype(BF).astype(F32)
        place = lax.broadcasted_iota(jnp.int32, (16, BLOCK), 0)
        pair = jnp.where(place == 0, top, jnp.where(place == 1, lam - top, 0.0)).astype(BF)
        at = pl.ds(pl.multiple_of(i * BLOCK, BLOCK), BLOCK)
        left[:features, at] = (x_ref[at, :].astype(F32).T * lam).astype(BF)
        left[features:, at] = pair

    pl.semaphore_wait(barrier, n - 1)

    def copy(source, target, send, recvs, peer, slot):
        return pltpu.make_async_remote_copy(
            src_ref=source,
            dst_ref=target.at[slot],
            send_sem=send,
            recv_sem=recvs.at[slot],
            device_id=(peer, core),
            device_id_type=MESH,
        )

    @pl.loop(0, groups)
    def _(k):
        for one in fetches(k):
            one.wait()

        @pl.when(k + 1 < groups)
        def _():
            for one in fetches(k + 1):
                one.start()

        group = lax.rem(first + k, groups)
        slot = lax.rem(k, 2)
        half_wo = wo_ref[group]
        sums = jnp.dot(left[...], g_buf[slot], preferred_element_type=F32)
        sums_o = jnp.dot(left[features:, :], h_buf[slot], preferred_element_type=F32)
        grad_b = jnp.sum(sums[features:], axis=0, keepdims=True) * half_wo
        grad_o = 0.5 * jnp.sum(sums_o, axis=0, keepdims=True)
        pieces = [
            (sums[:features] * half_wo).astype(BF),
            tail_rows(grad_b, grad_o),
        ]
        if padded > features + 16:
            pieces.append(jnp.zeros((padded - features - 16, WIDE), BF))
        block = jnp.concatenate(pieces, axis=0)
        for j in range(per_group):
            span, part = j // parts_per_span, j % parts_per_span
            parts[group * per_group + j] = block[
                part * chunk_rows : (part + 1) * chunk_rows, span * LANES : (span + 1) * LANES
            ]
        for j in range(per_group):
            owner = group * per_group + j

            @pl.when(owner != me)
            def _():
                copy(parts.at[owner], arrive, send_a.at[owner], recv_a, owner, me).start()

    def take(k, total):
        peer = lax.rem(me + n - k, n)
        copy(parts.at[peer], arrive, send_a.at[peer], recv_a, peer, peer).wait_recv()
        return total + arrive[peer].astype(F32)

    total = lax.fori_loop(1, n, take, parts[me].astype(F32))
    mine[...] = total.astype(BF)

    @pl.when(lax.rem(me, parts_per_span) == features // chunk_rows)
    def _():
        at = features % chunk_rows
        mine[at : at + 16, :] = tail_rows(
            total[at : at + 1] + total[at + 2 : at + 3],
            total[at + 1 : at + 2] + total[at + 3 : at + 4],
        )

    inner = 4
    outer = n // inner
    row, col = me // inner, lax.rem(me, inner)

    def outer_peer(i):
        return lax.rem(row + i, outer) * inner + col

    def inner_peer(j):
        return row * inner + lax.rem(col + j, inner)

    def send_outer(i):
        peer = outer_peer(i)
        return copy(mine, full, send_b.at[0, peer], recv_b, peer, me)

    def send_inner(j):
        return copy(mine, full, send_b.at[j, me], recv_b, inner_peer(j), me)

    def pass_on(i, j):
        chunk = outer_peer(outer - i)
        return copy(full.at[chunk], full, send_b.at[j, chunk], recv_b, inner_peer(j), chunk)

    def landed(chunk):
        return copy(mine, full, send_b.at[0, chunk], recv_b, me, chunk)

    for i in range(1, outer):
        send_outer(i).start()
    for j in range(1, inner):
        send_inner(j).start()
    out_ref[me] = mine[...]
    for i in range(1, outer):
        chunk = outer_peer(outer - i)
        landed(chunk).wait_recv()
        for j in range(1, inner):
            pass_on(i, j).start()
        out_ref[chunk] = full[chunk]
    for i in range(outer):
        for j in range(1, inner):
            chunk = lax.rem(row + outer - i, outer) * inner + lax.rem(col + j, inner)
            landed(chunk).wait_recv()
            out_ref[chunk] = full[chunk]

    @pl.loop(1, n)
    def _(k):
        peer = lax.rem(me + k, n)
        copy(parts.at[peer], arrive, send_a.at[peer], recv_a, peer, me).wait_send()

    for i in range(1, outer):
        send_outer(i).wait_send()
        for j in range(1, inner):
            pass_on(i, j).wait_send()
    for j in range(1, inner):
        send_inner(j).wait_send()


def gradients(n, rows, hid, slope, lam, wo_half, parts_per_span, chunk_rows):
    total, features = rows.shape
    groups = hid.shape[0]
    vmem = pl.BlockSpec(memory_space=pltpu.VMEM)
    hbm = pl.BlockSpec(memory_space=pl.ANY)
    shape = (n, chunk_rows, LANES)
    return pl.pallas_call(
        functools.partial(grad_kernel, n, parts_per_span),
        in_specs=[vmem, vmem, vmem, hbm, hbm],
        out_specs=vmem,
        out_shape=jax.ShapeDtypeStruct(shape, BF),
        scratch_shapes=[
            pltpu.VMEM((features + 16, total), BF),
            pltpu.VMEM((2, total, WIDE), BF),
            pltpu.VMEM((2, total, WIDE), BF),
            pltpu.VMEM(shape, BF),
            pltpu.VMEM(shape, BF),
            pltpu.VMEM(shape[1:], BF),
            pltpu.VMEM(shape, BF),
            pltpu.SemaphoreType.DMA((2, 2)),
            pltpu.SemaphoreType.DMA((n,)),
            pltpu.SemaphoreType.DMA((n,)),
            pltpu.SemaphoreType.DMA((4, n)),
            pltpu.SemaphoreType.DMA((n,)),
        ],
        compiler_params=pltpu.CompilerParams(
            collective_id=1, has_side_effects=True, vmem_limit_bytes=48 << 20
        ),
    )(rows, lam, wo_half, hid, slope)


def adam_step(weights, moment, second, gradient):
    moment_next = beta_one * moment + (1.0 - beta_one) * gradient
    second_next = beta_two * second + (1.0 - beta_two) * gradient * gradient
    weights_next = weights - learn_rate * moment_next / (jnp.sqrt(second_next) + adam_eps)
    return (weights_next, moment_next, second_next)


def adam_kernel(g_ref, w_ref, m_ref, s_ref, w_out, m_out, s_out):
    features = w_ref.shape[0]
    for k in range(g_ref.shape[0]):
        cols = slice(k * LANES, (k + 1) * LANES)
        grad = g_ref[k, :features, :].astype(F32)
        w_out[:, cols], m_out[:, cols], s_out[:, cols] = adam_step(
            w_ref[:, cols], m_ref[:, cols], s_ref[:, cols], grad
        )


def adam_matrix(grads, weights, moment, second):
    features, hidden = weights.shape
    group = 4
    block = pl.BlockSpec((features, group * LANES), lambda i: (0, i))
    return pl.pallas_call(
        adam_kernel,
        grid=(hidden // (group * LANES),),
        in_specs=[pl.BlockSpec((group,) + grads.shape[1:], lambda i: (i, 0, 0))] + [block] * 3,
        out_specs=[block] * 3,
        out_shape=[jax.ShapeDtypeStruct(weights.shape, F32)] * 3,
    )(grads, weights, moment, second)


def per_device(
    log_rows, query_ids, doc_ranks, row_counts, list_lengths, gains,
    weight_in, bias_in, weight_out, moment_w, second_w,
    moment_b, second_b, moment_o, second_o,
):
    n = lax.axis_size("dp")
    total, features = log_rows.shape
    cap = total // n
    hidden = weight_in.shape[1]
    list_count, list_width = gains.shape
    high_rows = list_count * list_width // LANES
    per_list = list_width // LANES

    is_live = jnp.arange(cap)[None, :] < row_counts.reshape(n, 1)
    slots = query_ids.reshape(n, cap) % list_count * list_width + doc_ranks.reshape(n, cap)
    high = jnp.where(is_live, slots // LANES, -1).astype(F32)
    low = (slots % LANES).astype(F32)

    positions = jnp.arange(list_width)
    discount = 1.0 / jnp.log2(2.0 + positions.astype(F32))
    weights = jnp.abs(discount[:, None] - discount[None, :]).reshape(per_list, LANES, list_width)
    keep = positions[None, :] < list_lengths[:, None]
    gain_rows = jnp.where(keep, gains, 0.0).reshape(high_rows, LANES)
    keep_rows = keep.astype(F32).reshape(high_rows, LANES)

    wo_half = 0.5 * weight_out
    wo_top = lax.reduce_precision(wo_half, exponent_bits=8, mantissa_bits=7)
    wo_rest = (wo_half - wo_top).astype(BF)
    wo_top = wo_top.astype(BF)
    lane = jnp.arange(LANES)[None, :]
    wo_pair = jnp.where(
        lane == 0, wo_top[:, None], jnp.where(lane == 1, wo_rest[:, None], jnp.zeros((), BF))
    )

    hid, slope, doc_rows, lam = score(
        n, lax.axis_size("mp"), log_rows, weight_in, bias_in.reshape(1, hidden), wo_pair,
        jnp.stack([high, low], axis=1), gain_rows, keep_rows, weights, list_count * n,
    )
    lambdas = doc_rows.reshape(list_count, list_width)

    spans = hidden // LANES
    row_parts = max(1, n // spans)
    unit = 16 * row_parts
    padded = (features + 16 + unit - 1) // unit * unit
    grads = gradients(
        n, log_rows, hid, slope, lam.reshape(total // BLOCK, 1, BLOCK),
        wo_half.reshape(hidden // WIDE, 1, WIDE), row_parts, padded // row_parts,
    )
    grads = grads.reshape(spans, padded, LANES)
    tail = grads[:, features : features + 4, :].astype(F32)
    grad_b = (tail[:, 0] + tail[:, 2]).reshape(hidden)
    grad_o = (tail[:, 1] + tail[:, 3]).reshape(hidden)
    return (
        lambdas,
        *adam_matrix(grads, weight_in, moment_w, second_w),
        *adam_step(bias_in, moment_b, second_b, grad_b),
        *adam_step(weight_out, moment_o, second_o, grad_o),
    )


def solution(mesh):
    dp, mp, both = P("dp"), P("mp"), P(None, "mp")
    rows = P("dp", None)
    return jax.shard_map(
        per_device,
        mesh=mesh,
        in_specs=(rows, dp, dp, rows, dp, rows, both, mp, mp, both, both, mp, mp, mp, mp),
        out_specs=(rows, both, both, both, mp, mp, mp, mp, mp, mp),
        check_vma=False,
    )
```
